128 devices in a mesh: grp: 8 (over z, x_hi), blk: 16 (over x_lo, y, core).
Axes of the slice: x: 4 (x_hi: 2, x_lo: 2; x = x_hi * 2 + x_lo), y: 4, z: 4, core: 2. Of those that a mesh axis runs over, the one named last changes fastest.
Arguments:
- slab: bfloat16 [32, 4096, 4096], P('grp', 'blk'), may hold values from -0.59765625 to 0.59765625
- block_mask: int32 [8, 128, 128], P('grp', 'blk'), may hold values 0 or 1
- orbitals: bfloat16 [4096, 1024], P('blk'), may hold values from -0.09375 to 0.09375
- margin: bfloat16 [4096, 4096], P('blk', 'grp'), as said below
- env_flag: int32 [1024], replicated, may hold values from 0 to 1
Outputs:
- projected: float32 [4096, 4096], P('blk', 'grp')
The draws below stay inside these ranges and needn't reach their ends.
Inputs may be any that keep to these rules, and one draw needn't show every extreme that they name: margin is symmetric positive definite with unit diagonal.
All inputs are finite; a program needn't handle non-finite values. No bound on the sum of `block_mask` on one device may be relied on, other than what follows from the above.
Results may differ from the reference program's by a relative error of at most 0.003.
Values may be sent and summed in bfloat16 or wider, within the bound.
No kernel may reach another device: no remote copies, remote signals or barrier semaphores. Data moves between devices by JAX's collectives and lax.ppermute only.
A program may use at most 128 MiB of HBM per device.

```python
import jax
import jax.numpy as jnp
from jax import lax

AUX_DEV = 4
OCC = 1024
ATILE = 32
NAO = 4096
AUX = 32
NAOB = 128
N_GRP = 8


def draw_margin(key, part):
    noise = jax.random.normal(key, (NAO, NAO), jnp.float32)
    sym = (noise + noise.T) * (0.25 / NAO ** 0.5)
    eye = jnp.eye(NAO, dtype=jnp.float32)
    return (eye + sym * (1.0 - eye)).astype(jnp.bfloat16)


def set_ends(result, rng, low, top_value):
    dims = result.shape
    place = [jax.random.randint(jax.random.fold_in(rng, axis), (), 0, dims[axis]) for axis in range(len(dims))]
    result = result.at[tuple(place)].set(low)
    longest = dims.index(max(dims))
    place[longest] = (place[longest] + 1) % dims[longest]
    return result.at[tuple(place)].set(top_value)


def block_levels(rng, extent, shards, smallest, high):
    gain = 1.0
    for axis_at, shards_of in shards:
        steps = jax.random.uniform(jax.random.fold_in(jax.random.fold_in(rng, 6), axis_at), (shards_of,), jnp.float32, smallest / len(shards), high / len(shards))
        gain = gain * jnp.repeat(jnp.exp(steps), extent[axis_at] // shards_of).reshape((-1,) + (1,) * (len(extent) - 1 - axis_at))
    return gain


def bell_draw(stream_key, extent, deviation, most, pieces=(), held_as=jnp.bfloat16):
    drawn = deviation * jax.random.normal(stream_key, extent, jnp.float32)
    if pieces:
        drawn = drawn * block_levels(stream_key, extent, pieces, -0.22, 0.18)
    return jnp.clip(drawn, -most, most).astype(held_as)


def setup_inputs(seed: int = 0) -> dict:
    key_of = jax.random.split(jax.random.key(seed), 6)
    return {
        "slab": bell_draw(key_of[0], (AUX, NAO, NAO), 0.1, 0.59765625, ((0, 8), (1, 16))),
        "block_mask": set_ends((jax.random.randint(key_of[1], (N_GRP, NAOB, NAOB), 0, 5) < 3).astype(jnp.int32), jax.random.fold_in(key_of[1], 1), 0, 1),
        "orbitals": bell_draw(key_of[2], (NAO, OCC), NAO ** -0.5, 0.09375, ((0, 16),)),
        "margin": draw_margin(jax.random.fold_in(key_of[5], 71), 0),
        "env_flag": set_ends(jax.random.randint(key_of[4], (OCC,), 0, 2), jax.random.fold_in(key_of[4], 1), 0, 1).astype(jnp.int32),
    }


def reference(slab, block_mask, orbitals, margin, env_flag):
    def transform(index):
        tiles = block_mask[index // AUX_DEV]
        keep_full = jnp.repeat(jnp.repeat(tiles, ATILE, axis=0), ATILE, axis=1).astype(jnp.bfloat16)
        masked = slab[index] * keep_full
        return jnp.dot(masked, orbitals, preferred_element_type=jnp.float32).astype(jnp.bfloat16)

    half = lax.map(transform, jnp.arange(AUX, dtype=jnp.int32))

    def accumulate(total, piece):
        return total + jnp.dot(piece, piece.T, preferred_element_type=jnp.float32), None

    exchange, unused = lax.scan(accumulate, jnp.zeros((NAO, NAO), jnp.float32), half)
    env_orbitals = orbitals * env_flag.astype(jnp.bfloat16)[None, :]
    exchange_bf = exchange.astype(jnp.bfloat16)
    left_env = jnp.dot(env_orbitals.T, exchange_bf, preferred_element_type=jnp.float32).astype(jnp.bfloat16)
    env_margin = jnp.dot(env_orbitals.T, margin, preferred_element_type=jnp.float32).astype(jnp.bfloat16)
    right_env = jnp.dot(exchange_bf, env_orbitals, preferred_element_type=jnp.float32).astype(jnp.bfloat16)
    margin_env = jnp.dot(margin, env_orbitals, preferred_element_type=jnp.float32).astype(jnp.bfloat16)
    first = jnp.dot(margin_env, left_env, preferred_element_type=jnp.float32)
    second = jnp.dot(right_env, env_margin, preferred_element_type=jnp.float32)
    return exchange - first - second
```

```python
import jax
import jax.numpy as jnp
from jax import lax
from jax.sharding import PartitionSpec as P

ATILE = 32
AXES = ("grp", "blk")
NZ, NH, NA, NY, NK = 4, 2, 2, 4, 2


def device(z, h, a, y, k):
    return ((z * NH + h) * NA + a) * NY * NK + y * NK + k


def moved(x, where):
    pairs = []
    for z in range(NZ):
        for h in range(NH):
            for a in range(NA):
                for y in range(NY):
                    for k in range(NK):
                        pairs.append((device(z, h, a, y, k), device(*where(z, h, a, y, k))))
    return lax.ppermute(x, AXES, pairs)


def from_next(x):
    return moved(x, lambda z, h, a, y, k: (z, h, a, (y - 1) % NY, k))


def from_prev(x):
    return moved(x, lambda z, h, a, y, k: (z, h, a, (y + 1) % NY, k))


def across_in(x):
    return moved(x, lambda z, h, a, y, k: (z, h, 1 - a, y, k))


def across_out(x):
    return moved(x, lambda z, h, a, y, k: (z, 1 - h, 1 - a, y, k))


def other_core(x):
    return moved(x, lambda z, h, a, y, k: (z, h, a, y, 1 - k))


def mirror(z, h, a, y, k):
    chip, group = a * NY + y, z * NH + h
    return (chip // NH, chip % NH, group // NY, group % NY, k)


def mirrored(x):
    return moved(x, mirror)


def mirrored_cross(x):
    def where(z, h, a, y, k):
        return mirror(z, h, a, y, 1 - k)

    return moved(x, where)


def to_absolute(rel, a, y):
    twice = jnp.concatenate([rel, rel], axis=1)
    turned = lax.dynamic_slice_in_dim(twice, (NY - y) % NY, NY, 1)
    return jnp.where(a == 0, turned, turned[::-1])


def tile_dot(left, right):
    return jnp.einsum("pmi,pni->mn", left, right, preferred_element_type=jnp.float32)


def gather_half(part):
    nxt, prv, acr = from_next(part), from_prev(part), across_in(part)
    mate = other_core(part)
    rows = jnp.concatenate([part, mate], axis=1)
    acr_nxt, acr_prv = from_next(acr), from_prev(acr)
    far0, far1 = from_next(nxt[:1]), from_prev(prv[1:])
    acr_far0, acr_far1 = across_in(far0), across_in(far1)
    early = [part, nxt, acr, prv]
    late = [acr_nxt, acr_prv, jnp.concatenate([far0, far1]), jnp.concatenate([acr_far0, acr_far1])]
    return rows, early + late


def summed_rows(tiles):
    wide = jnp.concatenate([t.astype(jnp.bfloat16) for t in tiles], axis=1)
    cols = wide.shape[1]
    cut = wide.reshape(2, 8, 32, cols).transpose(1, 0, 2, 3)
    got = lax.all_to_all(cut, "grp", 0, 0)
    total = got.astype(jnp.float32).sum(0)
    return [total[:, :, 256 * i : 256 * (i + 1)] for i in range(len(tiles))]


def on_device(slab, block_mask, orbitals, margin, env_flag):
    aux_dev, ao_dev, nao = slab.shape
    occ = orbitals.shape[1]
    blk = lax.axis_index("blk")
    chip, core = blk // NK, blk % NK
    a, y = chip // NY, chip % NY
    hb = ao_dev // 2

    margin_row = lax.all_gather(margin, "grp", axis=0)

    own = orbitals
    nxt, prv = from_next(own), from_prev(own)
    far = jnp.concatenate([from_next(nxt[:hb]), from_prev(prv[hb:])])
    near = [own, nxt, far, prv]
    cross = [jnp.concatenate([across_in(t[:hb]), across_out(t[hb:])]) for t in near]
    c_rel = jnp.stack(near + cross).reshape(NA, NY, ao_dev, occ)
    whole_c = jnp.zeros((NA, NY, NK, ao_dev, occ), jnp.bfloat16)
    for side, blocks in ((a, c_rel[:1]), (1 - a, c_rel[1:])):
        twice = jnp.concatenate([blocks, blocks], axis=1)
        mine = lax.dynamic_slice_in_dim(twice, (NY - y) % NY, NY, 1)[:, :, None]
        theirs = other_core(mine)
        whole_c = lax.dynamic_update_slice(whole_c, mine, (side, 0, core, 0, 0))
        whole_c = lax.dynamic_update_slice(whole_c, theirs, (side, 0, 1 - core, 0, 0))
    whole_c = whole_c.reshape(nao, occ)

    keep_tile = jnp.repeat(jnp.repeat(block_mask[0], ATILE, axis=0), ATILE, axis=1).astype(
        jnp.bfloat16
    )
    masked = slab * keep_tile[None, :, :]
    tiles = None
    for q in range(2):
        part = jnp.dot(
            masked[2 * q : 2 * q + 2].reshape(2 * ao_dev, nao),
            whole_c,
            preferred_element_type=jnp.float32,
        )
        part = part.astype(jnp.bfloat16).reshape(2, ao_dev, occ)
        rows, blocks = gather_half(part)
        new = [tile_dot(rows, b) for b in blocks]
        tiles = new if tiles is None else [t + n for t, n in zip(tiles, new)]

    flag = env_flag.astype(jnp.bfloat16)[None, :]
    ce_whole = whole_c * flag
    ce_rel = c_rel * flag
    a_rows = jnp.einsum(
        "gmn,gni->mi",
        margin_row,
        ce_whole.reshape(8, nao // 8, occ),
        preferred_element_type=jnp.float32,
    ).astype(jnp.bfloat16)
    a_own = mirrored(a_rows)
    a_oth = other_core(a_own)

    k00, k01, k10, k03 = summed_rows(tiles[:4])
    k11, k13, k02, k12 = summed_rows(tiles[4:])
    rel = jnp.stack([k00, k01, k02, k03, k10, k11, k12, k13])
    mine, theirs = rel[:, 0], other_core(rel[:, 1])
    k_rows = jnp.stack([mine, theirs], axis=2)
    k_bf = rel.astype(jnp.bfloat16)
    b_part = jnp.einsum(
        "tsmn,tni->smi",
        k_bf,
        ce_rel.reshape(8, ao_dev, occ),
        preferred_element_type=jnp.float32,
    )
    b_rows = (b_part[0] + other_core(b_part[1])).astype(jnp.bfloat16)
    k_abs = to_absolute(k_rows.reshape(NA, NY, 32, NK, ao_dev), a, y).reshape(8, 32, 512)
    hi = k_abs.astype(jnp.bfloat16)
    lo = (k_abs - hi.astype(jnp.float32)).astype(jnp.bfloat16)
    packed = jnp.concatenate(
        [jnp.broadcast_to(b_rows[None], (8, 32, occ)), hi, lo], axis=2
    )
    got = lax.all_to_all(packed, "grp", 0, 0).reshape(256, occ + 1024)
    b_all = got[:, :occ]
    k_tile = got[:, occ : occ + 512].astype(jnp.float32) + got[:, occ + 512 :].astype(jnp.float32)
    contract = (((1,), (1,)), ((), ()))
    z_own = lax.dot_general(b_all, a_own, contract, preferred_element_type=jnp.float32)
    z_oth = lax.dot_general(b_all, a_oth, contract, preferred_element_type=jnp.float32)
    t_own = mirrored(z_own.astype(jnp.bfloat16))
    t_oth = mirrored_cross(z_oth.astype(jnp.bfloat16))
    out_own = k_tile[:, :256] - z_own - t_own.astype(jnp.float32).T
    out_oth = k_tile[:, 256:] - z_oth - t_oth.astype(jnp.float32).T
    straight = jnp.concatenate([out_own, out_oth], axis=1)
    swapped = jnp.concatenate([out_oth, out_own], axis=1)
    return jnp.where(core == 0, straight, swapped)


def solution(mesh):
    placed = (P("grp", "blk", None), P("grp", "blk", None), P("blk", None), P("blk", "grp"), P())
    return jax.shard_map(
        on_device, mesh=mesh, in_specs=placed, out_specs=P("blk", "grp"), check_vma=False
    )
```

```python
import jax
import jax.numpy as jnp
from jax import lax
from jax.experimental import pallas as pl
from jax.experimental.pallas import tpu as pltpu
from jax.sharding import Mesh, PartitionSpec as P

ATILE = 32
AXES = ("grp", "chip", "core")
NZ, NH, NA, NY, NK = 4, 2, 2, 4, 2


def device(z, h, a, y, k):
    return ((z * NH + h) * NA + a) * NY * NK + y * NK + k


def moved(x, where):
    pairs = []
    for z in range(NZ):
        for h in range(NH):
            for a in range(NA):
                for y in range(NY):
                    for k in range(NK):
                        pairs.append((device(z, h, a, y, k), device(*where(z, h, a, y, k))))
    return lax.ppermute(x, AXES, pairs)


def from_next(x):
    return moved(x, lambda z, h, a, y, k: (z, h, a, (y - 1) % NY, k))


def from_prev(x):
    return moved(x, lambda z, h, a, y, k: (z, h, a, (y + 1) % NY, k))


def across_in(x):
    return moved(x, lambda z, h, a, y, k: (z, h, 1 - a, y, k))


def across_out(x):
    return moved(x, lambda z, h, a, y, k: (z, 1 - h, 1 - a, y, k))


def other_core(x):
    return moved(x, lambda z, h, a, y, k: (z, h, a, y, 1 - k))


def mirror(z, h, a, y, k):
    chip, group = a * NY + y, z * NH + h
    return (chip // NH, chip % NH, group // NY, group % NY, k)


def mirrored(x):
    return moved(x, mirror)


def mirrored_cross(x):
    def where(z, h, a, y, k):
        return mirror(z, h, a, y, 1 - k)

    return moved(x, where)


def to_absolute(rel, a, y):
    twice = jnp.concatenate([rel, rel], axis=1)
    turned = lax.dynamic_slice_in_dim(twice, (NY - y) % NY, NY, 1)
    return jnp.where(a == 0, turned, turned[::-1])


def after(x, *earlier):
    return lax.optimization_barrier((x,) + earlier)[0]


def masked_block(keep_ref, slab_ref):
    rows = slab_ref.shape[1]
    keep = keep_ref[...]
    wide = jnp.broadcast_to(keep[:, None, :], (keep.shape[0], ATILE, keep.shape[1]))
    wide = wide.reshape(rows, keep.shape[1]).astype(jnp.bfloat16)
    both = slab_ref[...] * wide[None]
    return both.reshape(slab_ref.shape[0] * rows, keep.shape[1])


def mask_kernel(cols, *refs):
    count = len(refs) // 3
    for at in range(count):
        refs[2 * count + at][...] = masked_block(refs[at], refs[count + at])


def masked_columns(cols, keep, slab, depth, steps):
    aux_dev, rows, nao = slab.shape
    count = nao // (depth * steps)
    keep_spec = [
        pl.BlockSpec((keep.shape[0], depth), lambda s, c, t=t: (0, c[t * steps + s]))
        for t in range(count)
    ]
    slab_spec = [
        pl.BlockSpec((aux_dev, rows, depth), lambda s, c, t=t: (0, 0, c[t * steps + s]))
        for t in range(count)
    ]
    return pl.pallas_call(
        mask_kernel,
        out_shape=[jax.ShapeDtypeStruct((aux_dev * rows, depth * steps), slab.dtype)] * count,
        grid_spec=pltpu.PrefetchScalarGridSpec(
            num_scalar_prefetch=1,
            grid=(steps,),
            in_specs=keep_spec + slab_spec,
            out_specs=[pl.BlockSpec((aux_dev * rows, depth), lambda s, c: (0, s))] * count,
        ),
        compiler_params=pltpu.CompilerParams(vmem_limit_bytes=40 << 20),
        name="masked_columns",
    )(cols, *[keep] * count, *[slab] * count)


def margin_kernel(cols, m1, m2, flag_ref, n1, n2, x1, x2, out_ref, acc):
    step = pl.program_id(0)
    half = pl.num_programs(0) // 2

    def add(c1, c2):
        left = jnp.concatenate([m1[0], m2[0]], axis=1)
        right = jnp.concatenate([c1[0], c2[0]], axis=0)
        acc[...] += jnp.dot(left, right, preferred_element_type=jnp.float32)

    @pl.when(step == 0)
    def _():
        acc[...] = jnp.zeros_like(acc)

    @pl.when(step < half)
    def _():
        add(n1, n2)

    @pl.when(step >= half)
    def _():
        add(x1, x2)

    @pl.when(step == pl.num_programs(0) - 1)
    def _():
        out_ref[...] = (acc[...] * flag_ref[...]).astype(out_ref.dtype)


def margin_env(cols, margin_row, flag, near, near_oth, cross, cross_oth):
    steps, depth, occ = near.shape
    rows = margin_row.shape[1]
    m_spec = [
        pl.BlockSpec(
            (1, rows, depth),
            lambda s, c, t=t: (c[t * 2 * steps + s] // NK, 0, c[t * 2 * steps + s] % NK),
        )
        for t in range(2)
    ]
    n_spec = pl.BlockSpec((1, depth, occ), lambda s, c: (jnp.minimum(s, steps - 1), 0, 0))
    x_spec = pl.BlockSpec((1, depth, occ), lambda s, c: (jnp.maximum(s - steps, 0), 0, 0))
    f_spec = pl.BlockSpec((1, occ), lambda s, c: (0, 0))
    return pl.pallas_call(
        margin_kernel,
        out_shape=jax.ShapeDtypeStruct((rows, occ), jnp.bfloat16),
        grid_spec=pltpu.PrefetchScalarGridSpec(
            num_scalar_prefetch=1,
            grid=(2 * steps,),
            in_specs=m_spec + [f_spec, n_spec, n_spec, x_spec, x_spec],
            out_specs=pl.BlockSpec((rows, occ), lambda s, c: (0, 0)),
            scratch_shapes=[pltpu.VMEM((rows, occ), jnp.float32)],
        ),
        compiler_params=pltpu.CompilerParams(vmem_limit_bytes=40 << 20),
        cost_estimate=pl.CostEstimate(
            flops=8 * rows * occ * depth * steps,
            transcendentals=0,
            bytes_accessed=8 * steps * depth * (rows + occ),
        ),
        name="margin_env",
    )(cols, margin_row, margin_row, flag, near, near_oth, cross, cross_oth)


def pair_kernel(core_ref, mine_ref, mate_ref, *refs):
    blocks, rest = refs[: len(refs) - 3], refs[len(refs) - 3 :]
    base_ref, out_ref, acc = rest
    run_pair(core_ref, mine_ref, mate_ref, blocks, base_ref, out_ref, acc)


def run_pair(core_ref, mine_ref, mate_ref, blocks, base_ref, out_ref, acc):
    step = pl.program_id(0)
    contract = (((1,), (1,)), ((), ()))
    left = jnp.concatenate([mine_ref[0], mate_ref[0]], axis=0)
    for at, block in enumerate(blocks):
        width = block.shape[1]
        cols = slice(at * width, (at + 1) * width)
        part = lax.dot_general(left, block[0], contract, preferred_element_type=jnp.float32)

        @pl.when(step == 0)
        def _():
            acc[:, cols] = part if base_ref is None else base_ref[:, cols] + part

        @pl.when(step > 0)
        def _():
            acc[:, cols] += part

    @pl.when(step == pl.num_programs(0) - 1)
    def _():
        if out_ref.shape == acc.shape:
            out_ref[...] = acc[...]
        else:
            core = core_ref[0]
            rows = mine_ref.shape[1]
            cut = out_ref.shape[:1] + out_ref.shape[2:]
            out_ref[:, core] = acc[:rows].reshape(cut).astype(out_ref.dtype)
            out_ref[:, 1 - core] = acc[rows:].reshape(cut).astype(out_ref.dtype)


def first_pair_kernel(core_ref, mine_ref, mate_ref, *refs):
    run_pair(core_ref, mine_ref, mate_ref, refs[:-2], None, refs[-2], refs[-1])


def pair_tiles(core, mine, mate, blocks, start=0, base=None, cut=True):
    depth, rows, occ = blocks[0].shape
    cols = rows * len(blocks)
    spec = pl.BlockSpec((1, rows, occ), lambda s, c: (s, 0, 0))
    own_spec = pl.BlockSpec((1, rows, occ), lambda s, c: (s + start, 0, 0))
    in_specs = [own_spec, own_spec] + [spec] * len(blocks)
    args = [core.reshape(1), mine, mate, *blocks]
    body = first_pair_kernel
    if base is not None:
        body = pair_kernel
        in_specs.append(pl.BlockSpec((2 * rows, cols), lambda s, c: (0, 0)))
        args.append(base)
    if cut:
        out = jax.ShapeDtypeStruct((8, 2, rows // 8, cols), jnp.bfloat16)
        out_spec = pl.BlockSpec(out.shape, lambda s, c: (0, 0, 0, 0))
    else:
        out = jax.ShapeDtypeStruct((2 * rows, cols), jnp.float32)
        out_spec = pl.BlockSpec(out.shape, lambda s, c: (0, 0))
    return pl.pallas_call(
        body,
        out_shape=out,
        grid_spec=pltpu.PrefetchScalarGridSpec(
            num_scalar_prefetch=1,
            grid=(depth,),
            in_specs=in_specs,
            out_specs=out_spec,
            scratch_shapes=[pltpu.VMEM((2 * rows, cols), jnp.float32)],
        ),
        compiler_params=pltpu.CompilerParams(vmem_limit_bytes=48 << 20),
        cost_estimate=pl.CostEstimate(
            flops=4 * rows * cols * depth * occ,
            transcendentals=0,
            bytes_accessed=2 * depth * occ * (2 * rows + cols) + 4 * rows * cols,
        ),
        name="exchange_tiles",
    )(*args)


def exchanged(cut):
    rows, cols = cut.shape[2:]
    return lax.all_to_all(cut.reshape(16, rows, cols), ("grp", "core"), 0, 0)


def sum_groups(got_ref, first):
    total = got_ref[first].astype(jnp.float32)
    for at in range(1, got_ref.shape[0] // 2):
        total += got_ref[2 * at + first].astype(jnp.float32)
    return total


def rows_times(rows, first, block):
    depth = block.shape[0]
    left = rows[:, first * depth : (first + 1) * depth].astype(jnp.bfloat16)
    return jnp.dot(left, block, preferred_element_type=jnp.float32)


def early_kernel(core_ref, got, near, near_oth, cross, cross_oth, k_ref, b_ref):
    core = core_ref[0]
    total = jnp.zeros(b_ref.shape, jnp.float32)
    for t, (nc, cc) in enumerate(((near, cross), (near_oth, cross_oth))):
        rows = sum_groups(got, core if t == 0 else 1 - core)
        k_ref[t] = rows
        for at, block in enumerate((nc[0], nc[1], nc[2], cc[0], nc[3])):
            total += rows_times(rows, at, block)
    b_ref[...] = total


def late_kernel(scalars, got, k_early, b_early, flag, cross, cross_oth, out_ref):
    core = scalars[0]
    occ = b_early.shape[1]
    depth = cross.shape[1]
    total = b_early[...]
    for t, cc in enumerate((cross, cross_oth)):
        rows = sum_groups(got, core if t == 0 else 1 - core)
        for at, block in enumerate((cc[3], cc[1], cc[2])):
            total += rows_times(rows, at, block)
        tiles = [k_early[t, :, at * depth : (at + 1) * depth] for at in range(5)]
        tiles += [rows[:, at * depth : (at + 1) * depth] for at in range(3)]
        first = occ + t * depth
        for at, place in enumerate((0, 1, 2, 4, 3, 7, 5, 6)):
            hi = tiles[at].astype(jnp.bfloat16)
            lo = (tiles[at] - hi.astype(jnp.float32)).astype(jnp.bfloat16)
            chip = scalars[1 + place]
            out_ref[chip, :, first : first + depth] = hi
            out_ref[chip, :, first + 2 * depth : first + 3 * depth] = lo
    b_rows = (total * flag[...]).astype(jnp.bfloat16)
    for at in range(out_ref.shape[0]):
        out_ref[at, :, :occ] = b_rows


def on_chip(body, name, out_shape, scalars, *args):
    flops = 4 * args[0].shape[1] * args[0].shape[2] * 1024
    return pl.pallas_call(
        body,
        out_shape=out_shape,
        in_specs=[pl.BlockSpec(memory_space=pltpu.SMEM)]
        + [pl.BlockSpec(memory_space=pltpu.VMEM)] * len(args),
        compiler_params=pltpu.CompilerParams(vmem_limit_bytes=40 << 20),
        cost_estimate=pl.CostEstimate(flops=flops, transcendentals=0, bytes_accessed=8 << 20),
        name=name,
    )(scalars, *args)


def early_rows(core, got, near, near_oth, cross, cross_oth):
    rows, cols = got.shape[1:]
    occ = near.shape[2]
    shapes = [
        jax.ShapeDtypeStruct((2, rows, cols), jnp.float32),
        jax.ShapeDtypeStruct((rows, occ), jnp.float32),
    ]
    args = (got, near, near_oth, cross, cross_oth)
    return on_chip(early_kernel, "early_rows", shapes, core.reshape(1), *args)


def late_rows(scalars, got, k_early, b_early, flag, cross, cross_oth):
    rows, occ = b_early.shape
    shape = jax.ShapeDtypeStruct((8, rows, occ + 4 * cross.shape[1]), jnp.bfloat16)
    args = (got, k_early, b_early, flag, cross, cross_oth)
    return on_chip(late_kernel, "late_rows", shape, scalars, *args)


def on_device(slab, block_mask, orbitals, margin, env_flag):
    aux_dev, ao_dev, nao = slab.shape
    occ = orbitals.shape[1]
    chip, core = lax.axis_index("chip"), lax.axis_index("core")
    a, y = chip // NY, chip % NY
    hb = ao_dev // 2
    flag = env_flag.astype(jnp.float32)[None, :]

    margin_row = lax.all_gather(margin, "grp", axis=0)
    order = (y + jnp.array([0, 1, NY - 1, 2], jnp.int32)) % NY
    near_cols = ((a * NY + order) * NK).astype(jnp.int32)
    cross_cols = (((1 - a) * NY + order) * NK).astype(jnp.int32)
    near_cols = jnp.concatenate([near_cols + core, near_cols + 1 - core])
    cross_cols = jnp.concatenate([cross_cols + core, cross_cols + 1 - core])
    keep = jnp.repeat(block_mask[0], ATILE, axis=1).astype(jnp.float32)
    masked = masked_columns(jnp.concatenate([near_cols, cross_cols]), keep, slab, ao_dev, NY)

    def product(left, right):
        return jnp.dot(left, right.reshape(-1, occ), preferred_element_type=jnp.float32)

    def cross_over(t):
        return [across_in(t[:hb]), across_out(t[hb:])]

    nxt, prv, *own_x, masked = lax.optimization_barrier(
        (from_next(orbitals), from_prev(orbitals), *cross_over(orbitals), masked)
    )
    far_lo, far_hi, *side_x = lax.optimization_barrier(
        (from_next(nxt[:hb]), from_prev(prv[hb:]), *cross_over(nxt), *cross_over(prv))
    )
    near = jnp.concatenate([orbitals, nxt, prv, far_lo, far_hi]).reshape(NY, ao_dev, occ)
    base = product(masked[0], near)
    near_oth, far_lo_x, far_hi_x, base = lax.optimization_barrier(
        (other_core(near), across_in(far_lo), across_out(far_hi), base)
    )
    cross = jnp.concatenate([*own_x, *side_x, far_lo_x, far_hi_x]).reshape(NY, ao_dev, occ)
    base += product(masked[1], near_oth)
    cross_oth, base = lax.optimization_barrier((other_core(cross), base))
    part = base + product(masked[2], cross) + product(masked[3], cross_oth)
    part = part.astype(jnp.bfloat16).reshape(aux_dev, ao_dev, occ)
    mid = aux_dev // 2

    x, n, p = across_in(part), from_next(part), from_prev(part)
    mate = other_core(part)
    gcols = jnp.concatenate([near_cols[:4], cross_cols[:4], near_cols[4:], cross_cols[4:]])
    a_rows = margin_env(gcols, margin_row, flag, after(near, mate), near_oth, cross, cross_oth)
    f, g = from_next(n[:mid]), from_prev(p[mid:])
    f, g, x, a_rows = lax.optimization_barrier((f, g, x, a_rows))
    xn, xp, xf = from_next(x), from_prev(x), across_in(f)
    xg = across_in(after(g, xf))

    far = jnp.concatenate([f, g])
    part_e, mate_e, _ = lax.optimization_barrier((part, mate, xf))
    early = pair_tiles(core, part_e, mate_e, [part, n, p, x, far])
    early = exchanged(early)
    k_early, b_early = early_rows(core, early, near, near_oth, cross, cross_oth)

    xfar = jnp.concatenate([xf, xg])
    late = pair_tiles(core, part, mate, [xfar, xn, xp])
    a_own = mirrored(after(a_rows, xn, xp))
    late, b_early, k_early, a_own = lax.optimization_barrier((late, b_early, k_early, a_own))
    late = exchanged(late)
    a_oth = other_core(a_own)
    places = jnp.concatenate([near_cols[:4], cross_cols[:4]]) // NK
    scalars = jnp.concatenate([core.reshape(1), places]).astype(jnp.int32)
    packed = late_rows(scalars, late, k_early, b_early, flag, cross, cross_oth)
    got = lax.all_to_all(packed, "grp", 0, 0).reshape(ao_dev, -1)
    b_all = got[:, :occ]
    k_tile = got[:, occ : occ + 512].astype(jnp.float32) + got[:, occ + 512 :].astype(jnp.float32)
    contract = (((1,), (1,)), ((), ()))
    z_own = lax.dot_general(b_all, a_own, contract, preferred_element_type=jnp.float32)
    z_oth = lax.dot_general(b_all, a_oth, contract, preferred_element_type=jnp.float32)
    t_own = mirrored(z_own.astype(jnp.bfloat16))
    t_oth = mirrored_cross(z_oth.astype(jnp.bfloat16))
    out_own = k_tile[:, :256] - z_own - t_own.astype(jnp.float32).T
    out_oth = k_tile[:, 256:] - z_oth - t_oth.astype(jnp.float32).T
    straight = jnp.concatenate([out_own, out_oth], axis=1)
    swapped = jnp.concatenate([out_oth, out_own], axis=1)
    return jnp.where(core == 0, straight, swapped)


def solution(mesh):
    fine = Mesh(mesh.devices.reshape(8, NA * NY, NK), AXES)
    blk = ("chip", "core")
    placed = (P("grp", blk, None), P("grp", blk, None), P(blk, None), P(blk, "grp"), P())
    return jax.shard_map(
        on_device, mesh=fine, in_specs=placed, out_specs=P(blk, "grp"), check_vma=False
    )
```

```python
import jax
import jax.numpy as jnp
from jax import lax
from jax.experimental import pallas as pl
from jax.experimental.pallas import tpu as pltpu
from jax.sharding import Mesh, PartitionSpec as P

ATILE = 32
AXES = ("grp", "chip", "core")
NZ, NH, NA, NY, NK = 4, 2, 2, 4, 2


def device(z, h, a, y, k):
    return ((z * NH + h) * NA + a) * NY * NK + y * NK + k


def moved(x, where):
    pairs = []
    for z in range(NZ):
        for h in range(NH):
            for a in range(NA):
                for y in range(NY):
                    for k in range(NK):
                        pairs.append((device(z, h, a, y, k), device(*where(z, h, a, y, k))))
    return lax.ppermute(x, AXES, pairs)


def from_next(x):
    return moved(x, lambda z, h, a, y, k: (z, h, a, (y - 1) % NY, k))


def from_prev(x):
    return moved(x, lambda z, h, a, y, k: (z, h, a, (y + 1) % NY, k))


def across_in(x):
    return moved(x, lambda z, h, a, y, k: (z, h, 1 - a, y, k))


def across_out(x):
    return moved(x, lambda z, h, a, y, k: (z, 1 - h, 1 - a, y, k))


def other_core(x):
    return moved(x, lambda z, h, a, y, k: (z, h, a, y, 1 - k))


def mirror(z, h, a, y, k):
    chip, group = a * NY + y, z * NH + h
    return (chip // NH, chip % NH, group // NY, group % NY, k)


def mirrored(x):
    return moved(x, mirror)


def mirrored_cross(x):
    def where(z, h, a, y, k):
        return mirror(z, h, a, y, 1 - k)

    return moved(x, where)


def to_absolute(rel, a, y):
    twice = jnp.concatenate([rel, rel], axis=1)
    turned = lax.dynamic_slice_in_dim(twice, (NY - y) % NY, NY, 1)
    return jnp.where(a == 0, turned, turned[::-1])


def after(x, *earlier):
    return lax.optimization_barrier((x,) + earlier)[0]


def masked_block(keep_ref, slab_ref):
    rows = slab_ref.shape[1]
    keep = keep_ref[...]
    wide = jnp.broadcast_to(keep[:, None, :], (keep.shape[0], ATILE, keep.shape[1]))
    wide = wide.reshape(rows, keep.shape[1]).astype(jnp.bfloat16)
    both = slab_ref[...] * wide[None]
    return both.reshape(slab_ref.shape[0] * rows, keep.shape[1])


def mask_kernel(cols, *refs):
    count = len(refs) // 3
    for at in range(count):
        refs[2 * count + at][...] = masked_block(refs[at], refs[count + at])


def masked_columns(cols, keep, slab, depth, steps):
    aux_dev, rows, nao = slab.shape
    count = nao // (depth * steps)
    keep_spec = [
        pl.BlockSpec((keep.shape[0], depth), lambda s, c, t=t: (0, c[t * steps + s]))
        for t in range(count)
    ]
    slab_spec = [
        pl.BlockSpec((aux_dev, rows, depth), lambda s, c, t=t: (0, 0, c[t * steps + s]))
        for t in range(count)
    ]
    return pl.pallas_call(
        mask_kernel,
        out_shape=[jax.ShapeDtypeStruct((aux_dev * rows, depth * steps), slab.dtype)] * count,
        grid_spec=pltpu.PrefetchScalarGridSpec(
            num_scalar_prefetch=1,
            grid=(steps,),
            in_specs=keep_spec + slab_spec,
            out_specs=[pl.BlockSpec((aux_dev * rows, depth), lambda s, c: (0, s))] * count,
        ),
        compiler_params=pltpu.CompilerParams(vmem_limit_bytes=40 << 20),
        name="masked_columns",
    )(cols, *[keep] * count, *[slab] * count)


def tiles_kernel(core_ref, *refs):
    pieces, out_ref = refs[:-1], refs[-1]
    rows = pieces[0].shape[1]
    contract = (((1,), (1,)), ((), ()))
    packs = []
    open_pack = []
    for piece in pieces:
        open_pack += [piece[at] for at in range(piece.shape[0])]
        if len(open_pack) == pieces[0].shape[0]:
            packs.append(jnp.concatenate(open_pack, axis=1))
            open_pack = []
    left = jnp.concatenate(packs[:2], axis=0)
    core = core_ref[0]
    for at, right in enumerate(packs[2:]):
        tile = lax.dot_general(left, right, contract, preferred_element_type=jnp.float32)
        tile = tile.astype(out_ref.dtype)
        cut = (out_ref.shape[0], out_ref.shape[2], rows)
        cols = slice(at * rows, (at + 1) * rows)
        out_ref[:, core, :, cols] = tile[:rows].reshape(cut)
        out_ref[:, 1 - core, :, cols] = tile[rows:].reshape(cut)


def pair_tiles(core, *pieces):
    depth, rows, occ = pieces[0].shape
    cols = rows * (sum(p.shape[0] for p in pieces) // depth - 2)
    specs = [pl.BlockSpec(p.shape, lambda s, c: (0, 0, 0)) for p in pieces]
    out = jax.ShapeDtypeStruct((8, 2, rows // 8, cols), jnp.bfloat16)
    return pl.pallas_call(
        tiles_kernel,
        out_shape=out,
        grid_spec=pltpu.PrefetchScalarGridSpec(
            num_scalar_prefetch=1,
            grid=(1,),
            in_specs=specs,
            out_specs=pl.BlockSpec(out.shape, lambda s, c: (0, 0, 0, 0)),
        ),
        compiler_params=pltpu.CompilerParams(vmem_limit_bytes=56 << 20),
        cost_estimate=pl.CostEstimate(
            flops=4 * rows * cols * depth * occ,
            transcendentals=0,
            bytes_accessed=2 * depth * occ * (2 * rows + cols) + 4 * rows * cols,
        ),
        name="exchange_tiles",
    )(core.reshape(1), *pieces)


def exchanged(cut):
    rows, cols = cut.shape[2:]
    return lax.all_to_all(cut.reshape(16, rows, cols), ("grp", "core"), 0, 0)


def sum_groups(got_ref, first):
    total = got_ref[first].astype(jnp.float32)
    for at in range(1, got_ref.shape[0] // 2):
        total += got_ref[2 * at + first].astype(jnp.float32)
    return total


def rows_times(rows, first, block):
    depth = block.shape[0]
    left = rows[:, first * depth : (first + 1) * depth].astype(jnp.bfloat16)
    return jnp.dot(left, block, preferred_element_type=jnp.float32)


def early_kernel(core_ref, got, near, near_oth, cross, cross_oth, k_ref, b_ref):
    core = core_ref[0]
    total = jnp.zeros(b_ref.shape, jnp.float32)
    for t, (nc, cc) in enumerate(((near, cross), (near_oth, cross_oth))):
        rows = sum_groups(got, core if t == 0 else 1 - core)
        k_ref[t] = rows
        for at, block in enumerate((nc[0], nc[1], nc[2], cc[0])):
            total += rows_times(rows, at, block)
    b_ref[...] = total


def late_kernel(scalars, got, k_early, b_early, flag, cross, cross_oth, far, out_ref):
    core = scalars[0]
    occ = b_early.shape[1]
    depth = cross.shape[1]
    total = b_early[...]
    tiles = []
    for t, cc in enumerate((cross, cross_oth)):
        rows = sum_groups(got, core if t == 0 else 1 - core)
        for at, block in enumerate((far[t], cc[3], cc[1], cc[2])):
            total += rows_times(rows, at, block)
        mine = [k_early[t, :, at * depth : (at + 1) * depth] for at in range(4)]
        tiles.append(mine + [rows[:, at * depth : (at + 1) * depth] for at in range(4)])
    for t in range(2):
        first = occ + t * depth
        for at, place in enumerate((0, 1, 2, 4, 3, 7, 5, 6)):
            tile = jnp.where(core == t, tiles[0][at], tiles[1][at])
            hi = tile.astype(jnp.bfloat16)
            lo = (tile - hi.astype(jnp.float32)).astype(jnp.bfloat16)
            chip = scalars[1 + place]
            out_ref[chip, :, first : first + depth] = hi
            out_ref[chip, :, first + 2 * depth : first + 3 * depth] = lo
    b_rows = (total * flag[...]).astype(jnp.bfloat16)
    for at in range(out_ref.shape[0]):
        out_ref[at, :, :occ] = b_rows


def on_chip(body, name, out_shape, scalars, *args):
    flops = 4 * args[0].shape[1] * args[0].shape[2] * 1024
    outs = out_shape if isinstance(out_shape, list) else [out_shape]

    def whole(array):
        zeros = (0,) * len(array.shape)
        return pl.BlockSpec(array.shape, lambda s, c: zeros)

    got = pl.pallas_call(
        body,
        out_shape=outs,
        grid_spec=pltpu.PrefetchScalarGridSpec(
            num_scalar_prefetch=1,
            grid=(1,),
            in_specs=[whole(a) for a in args],
            out_specs=[whole(o) for o in outs],
        ),
        compiler_params=pltpu.CompilerParams(vmem_limit_bytes=48 << 20),
        cost_estimate=pl.CostEstimate(flops=flops, transcendentals=0, bytes_accessed=8 << 20),
        name=name,
    )(scalars, *args)
    return got if isinstance(out_shape, list) else got[0]


def early_rows(core, got, near, near_oth, cross, cross_oth):
    rows, cols = got.shape[1:]
    occ = near.shape[2]
    shapes = [
        jax.ShapeDtypeStruct((2, rows, cols), jnp.float32),
        jax.ShapeDtypeStruct((rows, occ), jnp.float32),
    ]
    args = (got, near, near_oth, cross, cross_oth)
    return on_chip(early_kernel, "early_rows", shapes, core.reshape(1), *args)


def late_rows(scalars, got, k_early, b_early, flag, cross, cross_oth, far):
    rows, occ = b_early.shape
    shape = jax.ShapeDtypeStruct((8, rows, occ + 4 * cross.shape[1]), jnp.bfloat16)
    args = (got, k_early, b_early, flag, cross, cross_oth, far)
    return on_chip(late_kernel, "late_rows", shape, scalars, *args)


def on_device(slab, block_mask, orbitals, margin, env_flag):
    aux_dev, ao_dev, nao = slab.shape
    occ = orbitals.shape[1]
    chip, core = lax.axis_index("chip"), lax.axis_index("core")
    a, y = chip // NY, chip % NY
    hb = ao_dev // 2
    flag = env_flag.astype(jnp.float32)[None, :]

    a_part = lax.dot_general(
        margin, orbitals, (((0,), (0,)), ((), ())), preferred_element_type=jnp.float32
    )
    a_low, a_high = a_part[:ao_dev], a_part[ao_dev:]
    a_send = other_core(jnp.where(core == 0, a_high, a_low).astype(jnp.bfloat16))
    a_part = jnp.where(core == 0, a_low, a_high) + a_send.astype(jnp.float32)
    a_part = a_part.astype(jnp.bfloat16).reshape(8, 32, occ)
    order = (y + jnp.array([0, 1, NY - 1, 2], jnp.int32)) % NY
    near_cols = ((a * NY + order) * NK).astype(jnp.int32)
    cross_cols = (((1 - a) * NY + order) * NK).astype(jnp.int32)
    near_cols = jnp.concatenate([near_cols + core, near_cols + 1 - core])
    cross_cols = jnp.concatenate([cross_cols + core, cross_cols + 1 - core])
    keep = jnp.repeat(block_mask[0], ATILE, axis=1).astype(jnp.float32)
    masked = masked_columns(jnp.concatenate([near_cols, cross_cols]), keep, slab, ao_dev, NY)

    def product(left, right):
        return jnp.dot(left, right.reshape(-1, occ), preferred_element_type=jnp.float32)

    def cross_over(t):
        return [across_in(t[:hb]), across_out(t[hb:])]

    nxt, prv, *own_x, masked = lax.optimization_barrier(
        (from_next(orbitals), from_prev(orbitals), *cross_over(orbitals), masked)
    )
    far_lo, far_hi, a_part, *side_x = lax.optimization_barrier(
        (from_next(nxt[:hb]), from_prev(prv[hb:]), a_part, *cross_over(nxt), *cross_over(prv))
    )
    near = jnp.concatenate([orbitals, nxt, prv, far_lo, far_hi]).reshape(NY, ao_dev, occ)
    base = product(masked[0], near)
    near_oth, far_lo_x, far_hi_x, base = lax.optimization_barrier(
        (other_core(near), across_in(far_lo), across_out(far_hi), base)
    )
    cross = jnp.concatenate([*own_x, *side_x, far_lo_x, far_hi_x]).reshape(NY, ao_dev, occ)
    base += product(masked[1], near_oth)
    cross_oth, base = lax.optimization_barrier((other_core(cross), base))
    part = base + product(masked[2], cross) + product(masked[3], cross_oth)
    part = part.astype(jnp.bfloat16).reshape(aux_dev, ao_dev, occ)
    mid = aux_dev // 2

    x, n, p = across_in(part), from_next(part), from_prev(part)
    mate = other_core(part)
    a_got = lax.all_to_all(after(a_part, mate), "chip", 0, 0)
    a_slice = (a_got.astype(jnp.float32).sum(0) * flag).astype(jnp.bfloat16)
    a_slice = jnp.broadcast_to(a_slice[None], (8,) + a_slice.shape)
    a_own = lax.all_to_all(a_slice, "chip", 0, 0).reshape(ao_dev, occ)
    f, g = from_next(n[:mid]), from_prev(p[mid:])
    early = pair_tiles(core, part, mate, part, n, p, x)
    f, g, x, early, a_own = lax.optimization_barrier((f, g, x, early, a_own))
    a_oth = other_core(a_own)
    xn, xp = from_next(x), from_prev(x)
    xf, xg = across_in(f), across_in(g)
    early = exchanged(early)
    k_early, b_early = early_rows(core, early, near, near_oth, cross, cross_oth)

    late = exchanged(pair_tiles(core, part, mate, f, g, xf, xg, xn, xp))
    places = jnp.concatenate([near_cols[:4], cross_cols[:4]]) // NK
    scalars = jnp.concatenate([core.reshape(1), places]).astype(jnp.int32)
    far_c = jnp.stack([near[3], near_oth[3]])
    packed = late_rows(scalars, late, k_early, b_early, flag, cross, cross_oth, far_c)
    got = lax.all_to_all(packed, "grp", 0, 0).reshape(ao_dev, -1)
    b_all = got[:, :occ]
    k_tile = got[:, occ : occ + 512].astype(jnp.float32) + got[:, occ + 512 :].astype(jnp.float32)
    contract = (((1,), (1,)), ((), ()))
    z_own = lax.dot_general(b_all, a_own, contract, preferred_element_type=jnp.float32)
    z_oth = lax.dot_general(b_all, a_oth, contract, preferred_element_type=jnp.float32)
    t_own = mirrored(z_own.astype(jnp.bfloat16)).astype(jnp.float32).T + z_own
    t_oth = mirrored_cross(z_oth.astype(jnp.bfloat16)).astype(jnp.float32).T + z_oth
    low, high = jnp.where(core == 0, t_own, t_oth), jnp.where(core == 0, t_oth, t_own)
    return k_tile - jnp.concatenate([low, high], axis=1)


def solution(mesh):
    fine = Mesh(mesh.devices.reshape(8, NA * NY, NK), AXES)
    blk = ("chip", "core")
    placed = (P("grp", blk, None), P("grp", blk, None), P(blk, None), P(blk, "grp"), P())
    return jax.shard_map(
        on_device, mesh=fine, in_specs=placed, out_specs=P(blk, "grp"), check_vma=False
    )
```

```python
import jax
import jax.numpy as jnp
from jax import lax
from jax.experimental import pallas as pl
from jax.experimental.pallas import tpu as pltpu
from jax.sharding import Mesh, PartitionSpec as P

ATILE = 32
AXES = ("grp", "chip", "core")
NZ, NH, NA, NY, NK = 4, 2, 2, 4, 2


def device(z, h, a, y, k):
    return ((z * NH + h) * NA + a) * NY * NK + y * NK + k


def moved(x, where):
    pairs = []
    for z in range(NZ):
        for h in range(NH):
            for a in range(NA):
                for y in range(NY):
                    for k in range(NK):
                        pairs.append((device(z, h, a, y, k), device(*where(z, h, a, y, k))))
    return lax.ppermute(x, AXES, pairs)


def from_next(x):
    return moved(x, lambda z, h, a, y, k: (z, h, a, (y - 1) % NY, k))


def from_prev(x):
    return moved(x, lambda z, h, a, y, k: (z, h, a, (y + 1) % NY, k))


def across_in(x):
    return moved(x, lambda z, h, a, y, k: (z, h, 1 - a, y, k))


def across_out(x):
    return moved(x, lambda z, h, a, y, k: (z, 1 - h, 1 - a, y, k))


def other_core(x):
    return moved(x, lambda z, h, a, y, k: (z, h, a, y, 1 - k))


def mirror(z, h, a, y, k):
    chip, group = a * NY + y, z * NH + h
    return (chip // NH, chip % NH, group // NY, group % NY, k)


def mirrored(x):
    return moved(x, mirror)


def mirrored_cross(x):
    def where(z, h, a, y, k):
        return mirror(z, h, a, y, 1 - k)

    return moved(x, where)


def to_absolute(rel, a, y):
    twice = jnp.concatenate([rel, rel], axis=1)
    turned = lax.dynamic_slice_in_dim(twice, (NY - y) % NY, NY, 1)
    return jnp.where(a == 0, turned, turned[::-1])


def after(x, *earlier):
    return lax.optimization_barrier((x,) + earlier)[0]


def masked_block(keep_ref, slab_ref):
    rows = slab_ref.shape[1]
    keep = keep_ref[...]
    wide = jnp.broadcast_to(keep[:, None, :], (keep.shape[0], ATILE, keep.shape[1]))
    wide = wide.reshape(rows, keep.shape[1]).astype(jnp.bfloat16)
    both = slab_ref[...] * wide[None]
    return both.reshape(slab_ref.shape[0] * rows, keep.shape[1])


def mask_kernel(cols, *refs):
    count = len(refs) // 3
    for at in range(count):
        refs[2 * count + at][...] = masked_block(refs[at], refs[count + at])


def masked_columns(cols, keep, slab, depth, steps):
    aux_dev, rows, nao = slab.shape
    count = nao // (depth * steps)
    keep_spec = [
        pl.BlockSpec((keep.shape[0], depth), lambda s, c, t=t: (0, c[t * steps + s]))
        for t in range(count)
    ]
    slab_spec = [
        pl.BlockSpec((aux_dev, rows, depth), lambda s, c, t=t: (0, 0, c[t * steps + s]))
        for t in range(count)
    ]
    return pl.pallas_call(
        mask_kernel,
        out_shape=[jax.ShapeDtypeStruct((aux_dev * rows, depth * steps), slab.dtype)] * count,
        grid_spec=pltpu.PrefetchScalarGridSpec(
            num_scalar_prefetch=1,
            grid=(steps,),
            in_specs=keep_spec + slab_spec,
            out_specs=[pl.BlockSpec((aux_dev * rows, depth), lambda s, c: (0, s))] * count,
        ),
        compiler_params=pltpu.CompilerParams(vmem_limit_bytes=40 << 20),
        name="masked_columns",
    )(cols, *[keep] * count, *[slab] * count)


def tiles_kernel(core_ref, *refs):
    pieces, out_ref = refs[:-1], refs[-1]
    rows = pieces[0].shape[1]
    contract = (((1,), (1,)), ((), ()))
    packs = []
    open_pack = []
    for piece in pieces:
        open_pack += [piece[at] for at in range(piece.shape[0])]
        if len(open_pack) == pieces[0].shape[0]:
            packs.append(jnp.concatenate(open_pack, axis=1))
            open_pack = []
    left = jnp.concatenate(packs[:2], axis=0)
    core = core_ref[0]
    for at, right in enumerate(packs[2:]):
        tile = lax.dot_general(left, right, contract, preferred_element_type=jnp.float32)
        tile = tile.astype(out_ref.dtype)
        cut = (out_ref.shape[0], out_ref.shape[2], rows)
        cols = slice(at * rows, (at + 1) * rows)
        out_ref[:, core, :, cols] = tile[:rows].reshape(cut)
        out_ref[:, 1 - core, :, cols] = tile[rows:].reshape(cut)


def pair_tiles(core, *pieces):
    depth, rows, occ = pieces[0].shape
    cols = rows * (sum(p.shape[0] for p in pieces) // depth - 2)
    specs = [pl.BlockSpec(p.shape, lambda s, c: (0, 0, 0)) for p in pieces]
    out = jax.ShapeDtypeStruct((8, 2, rows // 8, cols), jnp.bfloat16)
    return pl.pallas_call(
        tiles_kernel,
        out_shape=out,
        grid_spec=pltpu.PrefetchScalarGridSpec(
            num_scalar_prefetch=1,
            grid=(1,),
            in_specs=specs,
            out_specs=pl.BlockSpec(out.shape, lambda s, c: (0, 0, 0, 0)),
        ),
        compiler_params=pltpu.CompilerParams(vmem_limit_bytes=56 << 20),
        cost_estimate=pl.CostEstimate(
            flops=4 * rows * cols * depth * occ,
            transcendentals=0,
            bytes_accessed=2 * depth * occ * (2 * rows + cols) + 4 * rows * cols,
        ),
        name="exchange_tiles",
    )(core.reshape(1), *pieces)


def exchanged(cut):
    rows, cols = cut.shape[2:]
    return lax.all_to_all(cut.reshape(16, rows, cols), ("grp", "core"), 0, 0)


def sum_groups(got_ref, first):
    total = got_ref[first].astype(jnp.float32)
    for at in range(1, got_ref.shape[0] // 2):
        total += got_ref[2 * at + first].astype(jnp.float32)
    return total


def rows_times(rows, first, block):
    depth = block.shape[0]
    left = rows[:, first * depth : (first + 1) * depth].astype(jnp.bfloat16)
    return jnp.dot(left, block, preferred_element_type=jnp.float32)


def early_kernel(core_ref, got, near, near_oth, cross, cross_oth, k_ref, b_ref):
    core = core_ref[0]
    total = jnp.zeros(b_ref.shape, jnp.float32)
    for t, (nc, cc) in enumerate(((near, cross), (near_oth, cross_oth))):
        rows = sum_groups(got, core if t == 0 else 1 - core)
        k_ref[t] = rows
        for at, block in enumerate((nc[0], nc[1], nc[2], cc[1], cc[0])):
            total += rows_times(rows, at, block)
    b_ref[...] = total


def late_kernel(scalars, got, k_early, b_early, flag, rest, rest_oth, out_ref):
    core = scalars[0]
    occ = b_early.shape[1]
    depth = rest.shape[1]
    total = b_early[...]
    tiles = []
    for t, cc in enumerate((rest, rest_oth)):
        rows = sum_groups(got, core if t == 0 else 1 - core)
        for at, block in enumerate((cc[4], cc[2], cc[3])):
            total += rows_times(rows, at, block)
        mine = [k_early[t, :, at * depth : (at + 1) * depth] for at in range(5)]
        tiles.append(mine + [rows[:, at * depth : (at + 1) * depth] for at in range(3)])
    for t in range(2):
        first = occ + t * depth
        for at, place in enumerate((0, 1, 2, 4, 3, 7, 5, 6)):
            tile = jnp.where(core == t, tiles[0][at], tiles[1][at])
            hi = tile.astype(jnp.bfloat16)
            lo = (tile - hi.astype(jnp.float32)).astype(jnp.bfloat16)
            chip = scalars[1 + place]
            out_ref[chip, :, first : first + depth] = hi
            out_ref[chip, :, first + 2 * depth : first + 3 * depth] = lo
    b_rows = (total * flag[...]).astype(jnp.bfloat16)
    for at in range(out_ref.shape[0]):
        out_ref[at, :, :occ] = b_rows


def on_chip(body, name, out_shape, scalars, *args):
    flops = 4 * args[0].shape[1] * args[0].shape[2] * 1024
    outs = out_shape if isinstance(out_shape, list) else [out_shape]

    def whole(array):
        zeros = (0,) * len(array.shape)
        return pl.BlockSpec(array.shape, lambda s, c: zeros)

    got = pl.pallas_call(
        body,
        out_shape=outs,
        grid_spec=pltpu.PrefetchScalarGridSpec(
            num_scalar_prefetch=1,
            grid=(1,),
            in_specs=[whole(a) for a in args],
            out_specs=[whole(o) for o in outs],
        ),
        compiler_params=pltpu.CompilerParams(vmem_limit_bytes=48 << 20),
        cost_estimate=pl.CostEstimate(flops=flops, transcendentals=0, bytes_accessed=8 << 20),
        name=name,
    )(scalars, *args)
    return got if isinstance(out_shape, list) else got[0]


def early_rows(core, got, near, near_oth, cross, cross_oth):
    rows, cols = got.shape[1:]
    occ = near.shape[2]
    shapes = [
        jax.ShapeDtypeStruct((2, rows, cols), jnp.float32),
        jax.ShapeDtypeStruct((rows, occ), jnp.float32),
    ]
    args = (got, near, near_oth, cross, cross_oth)
    return on_chip(early_kernel, "early_rows", shapes, core.reshape(1), *args)


def late_rows(scalars, got, k_early, b_early, flag, rest, rest_oth):
    rows, occ = b_early.shape
    shape = jax.ShapeDtypeStruct((8, rows, occ + 4 * rest.shape[1]), jnp.bfloat16)
    args = (got, k_early, b_early, flag, rest, rest_oth)
    return on_chip(late_kernel, "late_rows", shape, scalars, *args)


def on_device(slab, block_mask, orbitals, margin, env_flag):
    aux_dev, ao_dev, nao = slab.shape
    occ = orbitals.shape[1]
    chip, core = lax.axis_index("chip"), lax.axis_index("core")
    a, y = chip // NY, chip % NY
    hb = ao_dev // 2
    flag = env_flag.astype(jnp.float32)[None, :]

    a_part = lax.dot_general(
        margin, orbitals, (((0,), (0,)), ((), ())), preferred_element_type=jnp.float32
    )
    a_low, a_high = a_part[:ao_dev], a_part[ao_dev:]
    a_send = other_core(jnp.where(core == 0, a_high, a_low))
    order = (y + jnp.array([0, 1, NY - 1, 2], jnp.int32)) % NY
    sides = jnp.concatenate([a * NY + order, (1 - a) * NY + order]).astype(jnp.int32)
    cols = jnp.concatenate([sides * NK + core, sides * NK + 1 - core])
    keep = jnp.repeat(block_mask[0], ATILE, axis=1).astype(jnp.float32)
    own_m, oth_m = masked_columns(cols, keep, slab, ao_dev, NA * NY)
    wide = 3 * ao_dev

    def product(left, right):
        return jnp.dot(left, right.reshape(-1, occ), preferred_element_type=jnp.float32)

    def cross_over(t):
        return [across_in(t[:hb]), across_out(t[hb:])]

    nxt, prv, *own_x, own_m, oth_m = lax.optimization_barrier(
        (from_next(orbitals), from_prev(orbitals), *cross_over(orbitals), own_m, oth_m)
    )
    near = jnp.concatenate([orbitals, nxt, prv]).reshape(3, ao_dev, occ)
    base = product(own_m[:, :wide], near)
    far_lo, far_hi, side_in, side_out, near, base, a_send = lax.optimization_barrier(
        (
            from_next(nxt[:hb]),
            from_prev(prv[hb:]),
            across_in(jnp.concatenate([nxt[:hb], prv[:hb]])),
            across_out(jnp.concatenate([nxt[hb:], prv[hb:]])),
            near,
            base,
            a_send,
        )
    )
    side_x = [side_in[:hb], side_out[:hb], side_in[hb:], side_out[hb:]]
    far_x = [across_in(far_lo), across_out(far_hi)]
    near_oth = other_core(near)
    base += product(oth_m[:, :wide], near_oth)
    *far_x, base = lax.optimization_barrier((*far_x, base))
    rest = jnp.concatenate([far_lo, far_hi, *own_x, *side_x, *far_x]).reshape(5, ao_dev, occ)
    rest_oth = other_core(rest)
    base += product(own_m[:, wide:], rest)
    rest_oth, base = lax.optimization_barrier((rest_oth, base))
    part = base + product(oth_m[:, wide:], rest_oth)
    part = part.astype(jnp.bfloat16).reshape(aux_dev, ao_dev, occ)
    mid = aux_dev // 2

    x, n, p = across_in(part), from_next(part), from_prev(part)
    mate = other_core(part)
    a_send = after(a_send, mate)
    a_part = jnp.where(core == 0, a_low, a_high) + a_send
    a_part = a_part.astype(jnp.bfloat16).reshape(8, 32, occ)
    a_got = lax.all_to_all(a_part, "chip", 0, 0)
    a_slice = (a_got.astype(jnp.float32).sum(0) * flag).astype(jnp.bfloat16)
    a_slice = jnp.broadcast_to(a_slice[None], (8,) + a_slice.shape)
    a_own = lax.all_to_all(a_slice, "chip", 0, 0).reshape(ao_dev, occ)
    f, g = from_next(n[:mid]), from_prev(p[mid:])
    f, g, x, a_own = lax.optimization_barrier((f, g, x, a_own))
    a_oth = other_core(a_own)
    xn, xp = from_next(x), from_prev(x)
    xf, xg = across_in(f), across_in(g)
    early = exchanged(pair_tiles(core, part, mate, part, n, p, x, f, g))
    k_early, b_early = early_rows(core, early, near, near_oth, rest[:2], rest_oth[:2])

    late = exchanged(pair_tiles(core, part, mate, xf, xg, xn, xp))
    scalars = jnp.concatenate([core.reshape(1), sides]).astype(jnp.int32)
    packed = late_rows(scalars, late, k_early, b_early, flag, rest, rest_oth)
    got = lax.all_to_all(packed, "grp", 0, 0).reshape(ao_dev, -1)
    b_all = got[:, :occ]
    k_tile = got[:, occ : occ + 512].astype(jnp.float32) + got[:, occ + 512 :].astype(jnp.float32)
    contract = (((1,), (1,)), ((), ()))
    z_own = lax.dot_general(b_all, a_own, contract, preferred_element_type=jnp.float32)
    z_oth = lax.dot_general(b_all, a_oth, contract, preferred_element_type=jnp.float32)
    t_own = mirrored(z_own.astype(jnp.bfloat16)).astype(jnp.float32).T + z_own
    t_oth = mirrored_cross(z_oth.astype(jnp.bfloat16)).astype(jnp.float32).T + z_oth
    low, high = jnp.where(core == 0, t_own, t_oth), jnp.where(core == 0, t_oth, t_own)
    return k_tile - jnp.concatenate([low, high], axis=1)


def solution(mesh):
    fine = Mesh(mesh.devices.reshape(8, NA * NY, NK), AXES)
    blk = ("chip", "core")
    placed = (P("grp", blk, None), P("grp", blk, None), P(blk, None), P(blk, "grp"), P())
    return jax.shard_map(
        on_device, mesh=fine, in_specs=placed, out_specs=P(blk, "grp"), check_vma=False
    )
```

```python
import jax
import jax.numpy as jnp
from jax import lax
from jax.experimental import pallas as pl
from jax.experimental.pallas import tpu as pltpu
from jax.sharding import Mesh, PartitionSpec as P

ATILE = 32
AXES = ("grp", "chip", "core")
NZ, NH, NA, NY, NK = 4, 2, 2, 4, 2


def device(z, h, a, y, k):
    return ((z * NH + h) * NA + a) * NY * NK + y * NK + k


def moved(x, where):
    pairs = []
    for z in range(NZ):
        for h in range(NH):
            for a in range(NA):
                for y in range(NY):
                    for k in range(NK):
                        pairs.append((device(z, h, a, y, k), device(*where(z, h, a, y, k))))
    return lax.ppermute(x, AXES, pairs)


def from_next(x):
    return moved(x, lambda z, h, a, y, k: (z, h, a, (y - 1) % NY, k))


def from_prev(x):
    return moved(x, lambda z, h, a, y, k: (z, h, a, (y + 1) % NY, k))


def across_in(x):
    return moved(x, lambda z, h, a, y, k: (z, h, 1 - a, y, k))


def across_out(x):
    return moved(x, lambda z, h, a, y, k: (z, 1 - h, 1 - a, y, k))


def other_core(x):
    return moved(x, lambda z, h, a, y, k: (z, h, a, y, 1 - k))


def mirror(z, h, a, y, k):
    chip, group = a * NY + y, z * NH + h
    return (chip // NH, chip % NH, group // NY, group % NY, k)


def mirrored(x):
    return moved(x, mirror)


def mirrored_cross(x):
    def where(z, h, a, y, k):
        return mirror(z, h, a, y, 1 - k)

    return moved(x, where)


def to_absolute(rel, a, y):
    twice = jnp.concatenate([rel, rel], axis=1)
    turned = lax.dynamic_slice_in_dim(twice, (NY - y) % NY, NY, 1)
    return jnp.where(a == 0, turned, turned[::-1])


def after(x, *earlier):
    return lax.optimization_barrier((x,) + earlier)[0]


def masked_block(keep_ref, slab_ref):
    rows = slab_ref.shape[1]
    keep = keep_ref[...]
    wide = jnp.broadcast_to(keep[:, None, :], (keep.shape[0], ATILE, keep.shape[1]))
    wide = wide.reshape(rows, keep.shape[1]).astype(jnp.bfloat16)
    both = slab_ref[...] * wide[None]
    return both.reshape(slab_ref.shape[0] * rows, keep.shape[1])


def mask_kernel(cols, *refs):
    keeps, slabs, outs = refs[:4], refs[4:8], refs[8:]
    for at in range(4):
        depth = slabs[at].shape[2]
        place = slice((at % 2) * depth, (at % 2 + 1) * depth)
        outs[at // 2][:, place] = masked_block(keeps[at], slabs[at])


def masked_columns(cols, keep, slab, depth):
    aux_dev, rows, nao = slab.shape
    steps = nao // (4 * depth)
    firsts = [t * 2 * steps + u for t in range(2) for u in range(2)]
    keep_spec = [
        pl.BlockSpec((keep.shape[0], depth), lambda s, c, t=t: (0, c[t + 2 * s])) for t in firsts
    ]
    slab_spec = [
        pl.BlockSpec((aux_dev, rows, depth), lambda s, c, t=t: (0, 0, c[t + 2 * s]))
        for t in firsts
    ]
    return pl.pallas_call(
        mask_kernel,
        out_shape=[jax.ShapeDtypeStruct((aux_dev * rows, nao // 2), slab.dtype)] * 2,
        grid_spec=pltpu.PrefetchScalarGridSpec(
            num_scalar_prefetch=1,
            grid=(steps,),
            in_specs=keep_spec + slab_spec,
            out_specs=[pl.BlockSpec((aux_dev * rows, 2 * depth), lambda s, c: (0, s))] * 2,
        ),
        compiler_params=pltpu.CompilerParams(vmem_limit_bytes=40 << 20),
        name="masked_columns",
    )(cols, *[keep] * 4, *[slab] * 4)


def tiles_kernel(core_ref, *refs):
    pieces, out_ref = refs[:-1], refs[-1]
    rows = pieces[0].shape[1]
    contract = (((1,), (1,)), ((), ()))
    packs = []
    open_pack = []
    for piece in pieces:
        open_pack += [piece[at] for at in range(piece.shape[0])]
        if len(open_pack) == pieces[0].shape[0]:
            packs.append(jnp.concatenate(open_pack, axis=1))
            open_pack = []
    left = jnp.concatenate(packs[:2], axis=0)
    core = core_ref[0]
    for at, right in enumerate(packs[2:]):
        tile = lax.dot_general(left, right, contract, preferred_element_type=jnp.float32)
        tile = tile.astype(out_ref.dtype)
        cut = (out_ref.shape[0], out_ref.shape[2], rows)
        cols = slice(at * rows, (at + 1) * rows)
        out_ref[:, core, :, cols] = tile[:rows].reshape(cut)
        out_ref[:, 1 - core, :, cols] = tile[rows:].reshape(cut)


def pair_tiles(core, *pieces):
    depth, rows, occ = pieces[0].shape
    cols = rows * (sum(p.shape[0] for p in pieces) // depth - 2)
    specs = [pl.BlockSpec(p.shape, lambda s, c: (0, 0, 0)) for p in pieces]
    out = jax.ShapeDtypeStruct((8, 2, rows // 8, cols), jnp.bfloat16)
    return pl.pallas_call(
        tiles_kernel,
        out_shape=out,
        grid_spec=pltpu.PrefetchScalarGridSpec(
            num_scalar_prefetch=1,
            grid=(1,),
            in_specs=specs,
            out_specs=pl.BlockSpec(out.shape, lambda s, c: (0, 0, 0, 0)),
        ),
        compiler_params=pltpu.CompilerParams(vmem_limit_bytes=56 << 20),
        cost_estimate=pl.CostEstimate(
            flops=4 * rows * cols * depth * occ,
            transcendentals=0,
            bytes_accessed=2 * depth * occ * (2 * rows + cols) + 4 * rows * cols,
        ),
        name="exchange_tiles",
    )(core.reshape(1), *pieces)


def exchanged(cut):
    rows, cols = cut.shape[2:]
    return lax.all_to_all(cut.reshape(16, rows, cols), ("grp", "core"), 0, 0)


def sum_groups(got_ref, first):
    total = got_ref[first].astype(jnp.float32)
    for at in range(1, got_ref.shape[0] // 2):
        total += got_ref[2 * at + first].astype(jnp.float32)
    return total


def rows_times(rows, first, block):
    depth = block.shape[0]
    left = rows[:, first * depth : (first + 1) * depth].astype(jnp.bfloat16)
    return jnp.dot(left, block, preferred_element_type=jnp.float32)


def early_kernel(core_ref, got, near, near_oth, cross, cross_oth, k_ref, b_ref):
    core = core_ref[0]
    total = jnp.zeros(b_ref.shape, jnp.float32)
    for t, (nc, cc) in enumerate(((near, cross), (near_oth, cross_oth))):
        rows = sum_groups(got, core if t == 0 else 1 - core)
        k_ref[t] = rows
        for at, block in enumerate((nc[0], nc[1], nc[2], cc[1], cc[0])):
            total += rows_times(rows, at, block)
    b_ref[...] = total


def late_kernel(scalars, got, k_early, b_early, flag, rest, rest_oth, out_ref):
    core = scalars[0]
    occ = b_early.shape[1]
    depth = rest.shape[1]
    total = b_early[...]
    tiles = []
    for t, cc in enumerate((rest, rest_oth)):
        rows = sum_groups(got, core if t == 0 else 1 - core)
        for at, block in enumerate((cc[4], cc[2], cc[3])):
            total += rows_times(rows, at, block)
        mine = [k_early[t, :, at * depth : (at + 1) * depth] for at in range(5)]
        tiles.append(mine + [rows[:, at * depth : (at + 1) * depth] for at in range(3)])
    for t in range(2):
        first = occ + t * depth
        for at, place in enumerate((0, 1, 2, 4, 3, 7, 5, 6)):
            tile = jnp.where(core == t, tiles[0][at], tiles[1][at])
            hi = tile.astype(jnp.bfloat16)
            lo = (tile - hi.astype(jnp.float32)).astype(jnp.bfloat16)
            chip = scalars[1 + place]
            out_ref[chip, :, first : first + depth] = hi
            out_ref[chip, :, first + 2 * depth : first + 3 * depth] = lo
    b_rows = (total * flag[...]).astype(jnp.bfloat16)
    for at in range(out_ref.shape[0]):
        out_ref[at, :, :occ] = b_rows


def on_chip(body, name, out_shape, scalars, *args):
    flops = 4 * args[0].shape[1] * args[0].shape[2] * 1024
    outs = out_shape if isinstance(out_shape, list) else [out_shape]

    def whole(array):
        zeros = (0,) * len(array.shape)
        return pl.BlockSpec(array.shape, lambda s, c: zeros)

    got = pl.pallas_call(
        body,
        out_shape=outs,
        grid_spec=pltpu.PrefetchScalarGridSpec(
            num_scalar_prefetch=1,
            grid=(1,),
            in_specs=[whole(a) for a in args],
            out_specs=[whole(o) for o in outs],
        ),
        compiler_params=pltpu.CompilerParams(vmem_limit_bytes=48 << 20),
        cost_estimate=pl.CostEstimate(flops=flops, transcendentals=0, bytes_accessed=8 << 20),
        name=name,
    )(scalars, *args)
    return got if isinstance(out_shape, list) else got[0]


def early_rows(core, got, near, near_oth, cross, cross_oth):
    rows, cols = got.shape[1:]
    occ = near.shape[2]
    shapes = [
        jax.ShapeDtypeStruct((2, rows, cols), jnp.float32),
        jax.ShapeDtypeStruct((rows, occ), jnp.float32),
    ]
    args = (got, near, near_oth, cross, cross_oth)
    return on_chip(early_kernel, "early_rows", shapes, core.reshape(1), *args)


def late_rows(scalars, got, k_early, b_early, flag, rest, rest_oth):
    rows, occ = b_early.shape
    shape = jax.ShapeDtypeStruct((8, rows, occ + 4 * rest.shape[1]), jnp.bfloat16)
    args = (got, k_early, b_early, flag, rest, rest_oth)
    return on_chip(late_kernel, "late_rows", shape, scalars, *args)


def on_device(slab, block_mask, orbitals, margin, env_flag):
    aux_dev, ao_dev, nao = slab.shape
    occ = orbitals.shape[1]
    chip, core = lax.axis_index("chip"), lax.axis_index("core")
    a, y = chip // NY, chip % NY
    hb = ao_dev // 2
    flag = env_flag.astype(jnp.float32)[None, :]

    group = lax.axis_index("grp")
    row = (chip * NK + core) * ao_dev + lax.broadcasted_iota(jnp.int32, margin.shape, 0)
    col = group * 2 * ao_dev + lax.broadcasted_iota(jnp.int32, margin.shape, 1)
    margin_off = margin - (row == col).astype(margin.dtype)
    a_part = lax.dot_general(
        margin_off, orbitals, (((0,), (0,)), ((), ())), preferred_element_type=jnp.float32
    )
    a_low, a_high = a_part[:ao_dev], a_part[ao_dev:]
    a_send = other_core(jnp.where(core == 0, a_high, a_low))
    order = (y + jnp.array([0, 1, NY - 1, 2], jnp.int32)) % NY
    sides = jnp.concatenate([a * NY + order, (1 - a) * NY + order]).astype(jnp.int32)
    cols = jnp.concatenate([sides * NK + core, sides * NK + 1 - core])
    keep = jnp.repeat(block_mask[0], ATILE, axis=1).astype(jnp.float32)
    own_m, oth_m = masked_columns(cols, keep, slab, ao_dev)
    wide = 3 * ao_dev

    def product(left, right):
        return jnp.dot(left, right.reshape(-1, occ), preferred_element_type=jnp.float32)

    def cross_over(t):
        return [across_in(t[:hb]), across_out(t[hb:])]

    nxt, prv, *own_x, own_m, oth_m = lax.optimization_barrier(
        (from_next(orbitals), from_prev(orbitals), *cross_over(orbitals), own_m, oth_m)
    )
    near = jnp.concatenate([orbitals, nxt, prv]).reshape(3, ao_dev, occ)
    base = product(own_m[:, :wide], near)
    far_lo, far_hi, side_in, side_out, near, base, a_send = lax.optimization_barrier(
        (
            from_next(nxt[:hb]),
            from_prev(prv[hb:]),
            across_in(jnp.concatenate([nxt[:hb], prv[:hb]])),
            across_out(jnp.concatenate([nxt[hb:], prv[hb:]])),
            near,
            base,
            a_send,
        )
    )
    side_x = [side_in[:hb], side_out[:hb], side_in[hb:], side_out[hb:]]
    far_x = [across_in(far_lo), across_out(far_hi)]
    near_oth = other_core(near)
    base += product(oth_m[:, :wide], near_oth)
    *far_x, base = lax.optimization_barrier((*far_x, base))
    rest = jnp.concatenate([far_lo, far_hi, *own_x, *side_x, *far_x]).reshape(5, ao_dev, occ)
    rest_oth = other_core(rest)
    base += product(own_m[:, wide:], rest)
    rest_oth, base = lax.optimization_barrier((rest_oth, base))
    part = base + product(oth_m[:, wide:], rest_oth)
    part = part.astype(jnp.bfloat16).reshape(aux_dev, ao_dev, occ)
    mid = aux_dev // 2

    x, n, p = across_in(part), from_next(part), from_prev(part)
    mate = other_core(part)
    a_send = after(a_send, mate)
    a_part = jnp.where(core == 0, a_low, a_high) + a_send
    a_part = a_part.astype(jnp.bfloat16).reshape(8, 32, occ)
    a_got = lax.all_to_all(a_part, "chip", 0, 0)
    hit = (sides == group).astype(jnp.float32)[:, None, None]
    same = [lax.dynamic_slice_in_dim(t, chip * 32, 32, 1) for t in (near, rest)]
    same = (jnp.concatenate(same).astype(jnp.float32) * hit).sum(0)
    a_slice = ((a_got.astype(jnp.float32).sum(0) + same) * flag).astype(jnp.bfloat16)
    a_slice = jnp.broadcast_to(a_slice[None], (8,) + a_slice.shape)
    a_own = lax.all_to_all(a_slice, "chip", 0, 0).reshape(ao_dev, occ)
    f, g = from_next(n[:mid]), from_prev(p[mid:])
    f, g, x, a_own = lax.optimization_barrier((f, g, x, a_own))
    a_oth = other_core(a_own)
    xn, xp = from_next(x), from_prev(x)
    xf, xg = across_in(f), across_in(g)
    early = exchanged(pair_tiles(core, part, mate, part, n, p, x, f, g))
    k_early, b_early = early_rows(core, early, near, near_oth, rest[:2], rest_oth[:2])

    late = exchanged(pair_tiles(core, part, mate, xf, xg, xn, xp))
    scalars = jnp.concatenate([core.reshape(1), sides]).astype(jnp.int32)
    packed = late_rows(scalars, late, k_early, b_early, flag, rest, rest_oth)
    got = lax.all_to_all(packed, "grp", 0, 0).reshape(ao_dev, -1)
    b_all = got[:, :occ]
    k_tile = got[:, occ : occ + 512].astype(jnp.float32) + got[:, occ + 512 :].astype(jnp.float32)
    contract = (((1,), (1,)), ((), ()))
    z_own = lax.dot_general(b_all, a_own, contract, preferred_element_type=jnp.float32)
    z_oth = lax.dot_general(b_all, a_oth, contract, preferred_element_type=jnp.float32)
    t_own = mirrored(z_own.astype(jnp.bfloat16)).astype(jnp.float32).T + z_own
    t_oth = mirrored_cross(z_oth.astype(jnp.bfloat16)).astype(jnp.float32).T + z_oth
    low, high = jnp.where(core == 0, t_own, t_oth), jnp.where(core == 0, t_oth, t_own)
    return k_tile - jnp.concatenate([low, high], axis=1)


def solution(mesh):
    fine = Mesh(mesh.devices.reshape(8, NA * NY, NK), AXES)
    blk = ("chip", "core")
    placed = (P("grp", blk, None), P("grp", blk, None), P(blk, None), P(blk, "grp"), P())
    return jax.shard_map(
        on_device, mesh=fine, in_specs=placed, out_specs=P(blk, "grp"), check_vma=False
    )
```

```python
import jax
import jax.numpy as jnp
from jax import lax
from jax.experimental import pallas as pl
from jax.experimental.pallas import tpu as pltpu
from jax.sharding import Mesh, PartitionSpec as P

ATILE = 32
AXES = ("grp", "chip", "core")
NZ, NH, NA, NY, NK = 4, 2, 2, 4, 2


def device(z, h, a, y, k):
    return ((z * NH + h) * NA + a) * NY * NK + y * NK + k


def moved(x, where):
    pairs = []
    for z in range(NZ):
        for h in range(NH):
            for a in range(NA):
                for y in range(NY):
                    for k in range(NK):
                        pairs.append((device(z, h, a, y, k), device(*where(z, h, a, y, k))))
    return lax.ppermute(x, AXES, pairs)


def from_next(x):
    return moved(x, lambda z, h, a, y, k: (z, h, a, (y - 1) % NY, k))


def from_prev(x):
    return moved(x, lambda z, h, a, y, k: (z, h, a, (y + 1) % NY, k))


def across_in(x):
    return moved(x, lambda z, h, a, y, k: (z, h, 1 - a, y, k))


def across_out(x):
    return moved(x, lambda z, h, a, y, k: (z, 1 - h, 1 - a, y, k))


def other_core(x):
    return moved(x, lambda z, h, a, y, k: (z, h, a, y, 1 - k))


def mirror(z, h, a, y, k):
    chip, group = a * NY + y, z * NH + h
    return (chip // NH, chip % NH, group // NY, group % NY, k)


def mirrored(x):
    return moved(x, mirror)


def mirrored_cross(x):
    def where(z, h, a, y, k):
        return mirror(z, h, a, y, 1 - k)

    return moved(x, where)


def to_absolute(rel, a, y):
    twice = jnp.concatenate([rel, rel], axis=1)
    turned = lax.dynamic_slice_in_dim(twice, (NY - y) % NY, NY, 1)
    return jnp.where(a == 0, turned, turned[::-1])


def after(x, *earlier):
    return lax.optimization_barrier((x,) + earlier)[0]


def masked_block(keep_ref, slab_ref):
    rows = slab_ref.shape[1]
    keep = keep_ref[...]
    wide = jnp.broadcast_to(keep[:, None, :], (keep.shape[0], ATILE, keep.shape[1]))
    wide = wide.reshape(rows, keep.shape[1]).astype(jnp.bfloat16)
    both = slab_ref[...] * wide[None]
    return both.reshape(slab_ref.shape[0] * rows, keep.shape[1])


def mask_kernel(cols, *refs):
    keeps, slabs, outs = refs[:4], refs[4:8], refs[8:]
    for at in range(4):
        depth = slabs[at].shape[2]
        place = slice((at % 2) * depth, (at % 2 + 1) * depth)
        outs[at // 2][:, place] = masked_block(keeps[at], slabs[at])


def masked_columns(cols, keep, slab, depth):
    aux_dev, rows, nao = slab.shape
    steps = nao // (4 * depth)
    firsts = [t * 2 * steps + u for t in range(2) for u in range(2)]
    keep_spec = [
        pl.BlockSpec((keep.shape[0], depth), lambda s, c, t=t: (0, c[t + 2 * s])) for t in firsts
    ]
    slab_spec = [
        pl.BlockSpec((aux_dev, rows, depth), lambda s, c, t=t: (0, 0, c[t + 2 * s]))
        for t in firsts
    ]
    return pl.pallas_call(
        mask_kernel,
        out_shape=[jax.ShapeDtypeStruct((aux_dev * rows, nao // 2), slab.dtype)] * 2,
        grid_spec=pltpu.PrefetchScalarGridSpec(
            num_scalar_prefetch=1,
            grid=(steps,),
            in_specs=keep_spec + slab_spec,
            out_specs=[pl.BlockSpec((aux_dev * rows, 2 * depth), lambda s, c: (0, s))] * 2,
        ),
        compiler_params=pltpu.CompilerParams(vmem_limit_bytes=40 << 20),
        name="masked_columns",
    )(cols, *[keep] * 4, *[slab] * 4)


def tiles_kernel(core_ref, *refs):
    pieces, out_ref = refs[:-1], refs[-1]
    rows = pieces[0].shape[1]
    contract = (((1,), (1,)), ((), ()))
    packs = []
    open_pack = []
    for piece in pieces:
        open_pack += [piece[at] for at in range(piece.shape[0])]
        if len(open_pack) == pieces[0].shape[0]:
            packs.append(jnp.concatenate(open_pack, axis=1))
            open_pack = []
    left = jnp.concatenate(packs[:2], axis=0)
    core = core_ref[0]
    for at, right in enumerate(packs[2:]):
        tile = lax.dot_general(left, right, contract, preferred_element_type=jnp.float32)
        tile = tile.astype(out_ref.dtype)
        cut = (out_ref.shape[0], out_ref.shape[2], rows)
        cols = slice(at * rows, (at + 1) * rows)
        out_ref[:, core, :, cols] = tile[:rows].reshape(cut)
        out_ref[:, 1 - core, :, cols] = tile[rows:].reshape(cut)


def pair_tiles(core, *pieces):
    depth, rows, occ = pieces[0].shape
    cols = rows * (sum(p.shape[0] for p in pieces) // depth - 2)
    specs = [pl.BlockSpec(p.shape, lambda s, c: (0, 0, 0)) for p in pieces]
    out = jax.ShapeDtypeStruct((8, 2, rows // 8, cols), jnp.bfloat16)
    return pl.pallas_call(
        tiles_kernel,
        out_shape=out,
        grid_spec=pltpu.PrefetchScalarGridSpec(
            num_scalar_prefetch=1,
            grid=(1,),
            in_specs=specs,
            out_specs=pl.BlockSpec(out.shape, lambda s, c: (0, 0, 0, 0)),
        ),
        compiler_params=pltpu.CompilerParams(vmem_limit_bytes=56 << 20),
        cost_estimate=pl.CostEstimate(
            flops=4 * rows * cols * depth * occ,
            transcendentals=0,
            bytes_accessed=2 * depth * occ * (2 * rows + cols) + 4 * rows * cols,
        ),
        name="exchange_tiles",
    )(core.reshape(1), *pieces)


def exchanged(cut):
    rows, cols = cut.shape[2:]
    return lax.all_to_all(cut.reshape(16, rows, cols), ("grp", "core"), 0, 0)


def sum_groups(got_ref, first):
    total = got_ref[first].astype(jnp.float32)
    for at in range(1, got_ref.shape[0] // 2):
        total += got_ref[2 * at + first].astype(jnp.float32)
    return total


def rows_times(rows, first, block):
    depth = block.shape[0]
    left = rows[:, first * depth : (first + 1) * depth].astype(jnp.bfloat16)
    return jnp.dot(left, block, preferred_element_type=jnp.float32)


def early_kernel(core_ref, got, near, near_oth, cross, cross_oth, k_ref, b_ref):
    core = core_ref[0]
    total = jnp.zeros(b_ref.shape, jnp.float32)
    for t, (nc, cc) in enumerate(((near, cross), (near_oth, cross_oth))):
        rows = sum_groups(got, core if t == 0 else 1 - core)
        k_ref[t] = rows
        for at, block in enumerate((nc[0], nc[1], nc[2], cc[1], cc[0])):
            total += rows_times(rows, at, block)
    b_ref[...] = total


def late_kernel(scalars, got, k_early, b_early, flag, rest, rest_oth, out_ref):
    core = scalars[0]
    occ = b_early.shape[1]
    depth = rest.shape[1]
    total = b_early[...]
    tiles = []
    for t, cc in enumerate((rest, rest_oth)):
        rows = sum_groups(got, core if t == 0 else 1 - core)
        for at, block in enumerate((cc[4], cc[2], cc[3])):
            total += rows_times(rows, at, block)
        mine = [k_early[t, :, at * depth : (at + 1) * depth] for at in range(5)]
        tiles.append(mine + [rows[:, at * depth : (at + 1) * depth] for at in range(3)])
    for t in range(2):
        first = occ + t * depth
        for at, place in enumerate((0, 1, 2, 4, 3, 7, 5, 6)):
            tile = jnp.where(core == t, tiles[0][at], tiles[1][at])
            hi = tile.astype(jnp.bfloat16)
            lo = (tile - hi.astype(jnp.float32)).astype(jnp.bfloat16)
            chip = scalars[1 + place]
            out_ref[chip, :, first : first + depth] = hi
            out_ref[chip, :, first + 2 * depth : first + 3 * depth] = lo
    b_rows = (total * flag[...]).astype(jnp.bfloat16)
    for at in range(out_ref.shape[0]):
        out_ref[at, :, :occ] = b_rows


def on_chip(body, name, out_shape, scalars, *args):
    flops = 4 * args[0].shape[1] * args[0].shape[2] * 1024
    outs = out_shape if isinstance(out_shape, list) else [out_shape]

    def whole(array):
        zeros = (0,) * len(array.shape)
        return pl.BlockSpec(array.shape, lambda s, c: zeros)

    got = pl.pallas_call(
        body,
        out_shape=outs,
        grid_spec=pltpu.PrefetchScalarGridSpec(
            num_scalar_prefetch=1,
            grid=(1,),
            in_specs=[whole(a) for a in args],
            out_specs=[whole(o) for o in outs],
        ),
        compiler_params=pltpu.CompilerParams(vmem_limit_bytes=48 << 20),
        cost_estimate=pl.CostEstimate(flops=flops, transcendentals=0, bytes_accessed=8 << 20),
        name=name,
    )(scalars, *args)
    return got if isinstance(out_shape, list) else got[0]


def early_rows(core, got, near, near_oth, cross, cross_oth):
    rows, cols = got.shape[1:]
    occ = near.shape[2]
    shapes = [
        jax.ShapeDtypeStruct((2, rows, cols), jnp.float32),
        jax.ShapeDtypeStruct((rows, occ), jnp.float32),
    ]
    args = (got, near, near_oth, cross, cross_oth)
    return on_chip(early_kernel, "early_rows", shapes, core.reshape(1), *args)


def late_rows(scalars, got, k_early, b_early, flag, rest, rest_oth):
    rows, occ = b_early.shape
    shape = jax.ShapeDtypeStruct((8, rows, occ + 4 * rest.shape[1]), jnp.bfloat16)
    args = (got, k_early, b_early, flag, rest, rest_oth)
    return on_chip(late_kernel, "late_rows", shape, scalars, *args)


def on_device(slab, block_mask, orbitals, margin, env_flag):
    aux_dev, ao_dev, nao = slab.shape
    occ = orbitals.shape[1]
    chip, core = lax.axis_index("chip"), lax.axis_index("core")
    a, y = chip // NY, chip % NY
    hb = ao_dev // 2
    flag = env_flag.astype(jnp.float32)[None, :]

    order = (y + jnp.array([0, 1, NY - 1, 2], jnp.int32)) % NY
    sides = jnp.concatenate([a * NY + order, (1 - a) * NY + order]).astype(jnp.int32)
    cols = jnp.concatenate([sides * NK + core, sides * NK + 1 - core])
    keep = jnp.repeat(block_mask[0], ATILE, axis=1).astype(jnp.float32)
    own_m, oth_m = masked_columns(cols, keep, slab, ao_dev)
    wide = 3 * ao_dev

    def product(left, right):
        return jnp.dot(left, right.reshape(-1, occ), preferred_element_type=jnp.float32)

    def cross_over(t):
        return [across_in(t[:hb]), across_out(t[hb:])]

    nxt, prv, margin, *own_x, own_m, oth_m = lax.optimization_barrier(
        (from_next(orbitals), from_prev(orbitals), margin, *cross_over(orbitals), own_m, oth_m)
    )
    group = lax.axis_index("grp")
    row = (chip * NK + core) * ao_dev + lax.broadcasted_iota(jnp.int32, margin.shape, 0)
    col = group * 2 * ao_dev + lax.broadcasted_iota(jnp.int32, margin.shape, 1)
    margin_off = margin - (row == col).astype(margin.dtype)
    a_part = lax.dot_general(
        margin_off, orbitals, (((0,), (0,)), ((), ())), preferred_element_type=jnp.float32
    )
    a_low, a_high = a_part[:ao_dev], a_part[ao_dev:]
    a_send = other_core(jnp.where(core == 0, a_high, a_low))
    near = jnp.concatenate([orbitals, nxt, prv]).reshape(3, ao_dev, occ)
    base = product(own_m[:, :wide], near)
    far_lo, far_hi, side_in, side_out, near, base, a_send = lax.optimization_barrier(
        (
            from_next(nxt[:hb]),
            from_prev(prv[hb:]),
            across_in(jnp.concatenate([nxt[:hb], prv[:hb]])),
            across_out(jnp.concatenate([nxt[hb:], prv[hb:]])),
            near,
            base,
            a_send,
        )
    )
    side_x = [side_in[:hb], side_out[:hb], side_in[hb:], side_out[hb:]]
    far_x = [across_in(far_lo), across_out(far_hi)]
    near_oth = other_core(near)
    base += product(oth_m[:, :wide], near_oth)
    *far_x, base = lax.optimization_barrier((*far_x, base))
    rest = jnp.concatenate([far_lo, far_hi, *own_x, *side_x, *far_x]).reshape(5, ao_dev, occ)
    rest_oth = other_core(rest)
    base += product(own_m[:, wide:], rest)
    rest_oth, base = lax.optimization_barrier((rest_oth, base))
    part = base + product(oth_m[:, wide:], rest_oth)
    part = part.astype(jnp.bfloat16).reshape(aux_dev, ao_dev, occ)
    mid = aux_dev // 2

    x, n, p = across_in(part), from_next(part), from_prev(part)
    mate = other_core(part)
    a_send = after(a_send, mate)
    a_part = jnp.where(core == 0, a_low, a_high) + a_send
    a_part = a_part.astype(jnp.bfloat16).reshape(8, 32, occ)
    a_got = lax.all_to_all(a_part, "chip", 0, 0)
    hit = (sides == group).astype(jnp.float32)[:, None, None]
    same = [lax.dynamic_slice_in_dim(t, chip * 32, 32, 1) for t in (near, rest)]
    same = (jnp.concatenate(same).astype(jnp.float32) * hit).sum(0)
    a_slice = ((a_got.astype(jnp.float32).sum(0) + same) * flag).astype(jnp.bfloat16)
    a_slice = jnp.broadcast_to(a_slice[None], (8,) + a_slice.shape)
    a_own = lax.all_to_all(a_slice, "chip", 0, 0).reshape(ao_dev, occ)
    f, g = from_next(n[:mid]), from_prev(p[mid:])
    f, g, x, a_own = lax.optimization_barrier((f, g, x, a_own))
    a_oth = other_core(a_own)
    xn, xp = from_next(x), from_prev(x)
    xf, xg = across_in(f), across_in(g)
    early = exchanged(pair_tiles(core, part, mate, part, n, p, x, f, g))
    k_early, b_early = early_rows(core, early, near, near_oth, rest[:2], rest_oth[:2])

    late = exchanged(pair_tiles(core, part, mate, xf, xg, xn, xp))
    scalars = jnp.concatenate([core.reshape(1), sides]).astype(jnp.int32)
    packed = late_rows(scalars, late, k_early, b_early, flag, rest, rest_oth)
    got = lax.all_to_all(packed, "grp", 0, 0).reshape(ao_dev, -1)
    b_all = got[:, :occ]
    k_tile = got[:, occ : occ + 512].astype(jnp.float32) + got[:, occ + 512 :].astype(jnp.float32)
    contract = (((1,), (1,)), ((), ()))
    z_own = lax.dot_general(b_all, a_own, contract, preferred_element_type=jnp.float32)
    z_oth = lax.dot_general(b_all, a_oth, contract, preferred_element_type=jnp.float32)
    t_own = mirrored(z_own.astype(jnp.bfloat16)).astype(jnp.float32).T + z_own
    t_oth = mirrored_cross(z_oth.astype(jnp.bfloat16)).astype(jnp.float32).T + z_oth
    low, high = jnp.where(core == 0, t_own, t_oth), jnp.where(core == 0, t_oth, t_own)
    return k_tile - jnp.concatenate([low, high], axis=1)


def solution(mesh):
    fine = Mesh(mesh.devices.reshape(8, NA * NY, NK), AXES)
    blk = ("chip", "core")
    placed = (P("grp", blk, None), P("grp", blk, None), P(blk, None), P(blk, "grp"), P())
    return jax.shard_map(
        on_device, mesh=fine, in_specs=placed, out_specs=P(blk, "grp"), check_vma=False
    )
```
